32 devices in a mesh: ctx: 8 (over y, x, core), fsdp: 4 (over z).
Axes of the slice: x: 2, y: 2, z: 4, core: 2. Of those that a mesh axis runs over, the one named last changes fastest.
Arguments:
- inputs: bfloat16 [4, 2048, 768], P('fsdp', 'ctx'), may hold values from -6 to 6
- gain_attn: bfloat16 [768], P('fsdp'), may hold values from 0.5 to 1.5
- w_qkv: bfloat16 [768, 2304], P('fsdp'), may hold values from -0.21875 to 0.21875
- w_out: bfloat16 [768, 768], P('fsdp'), may hold values from -1.75 to 1.75
- gain_ffn: bfloat16 [768], P('fsdp'), may hold values from 0.5 to 1.5
- w_shared_in: bfloat16 [768, 4096], P('fsdp'), may hold values from -0.21875 to 0.21875
- w_shared_down: bfloat16 [2048, 768], P('fsdp'), may hold values from -0.125 to 0.125
- w_expert_in: bfloat16 [16, 768, 4096], P('fsdp'), may hold values from -0.21875 to 0.21875
- w_expert_down: bfloat16 [16, 2048, 768], P('fsdp'), may hold values from -0.125 to 0.125
- lengths: int32 [4], P('fsdp'), may hold values from 512 to 2048, as said below
- routes: int32 [4, 2048, 2], P('fsdp', 'ctx'), may hold values from 0 to 15, all different within a row; in each aligned block of 256 rows (0 to 255, 256 to 511, ..., all dimensions but the last counted through in order) at most 64 rows name the same one
- gates: float32 [4, 2048, 2], P('fsdp', 'ctx'), may hold values from 0.2 to 1
- cotangent: bfloat16 [4, 2048, 768], P('fsdp', 'ctx'), may hold values from -6 to 6
Outputs:
- output: bfloat16 [4, 2048, 768], P('fsdp', 'ctx')
- grad_inputs: float32 [4, 2048, 768], P('fsdp', 'ctx')
- grad_gain_attn: float32 [768], P('fsdp')
- grad_qkv: float32 [768, 2304], P('fsdp', 'ctx')
- grad_out: float32 [768, 768], P('fsdp', 'ctx')
- grad_gain_ffn: float32 [768], P('fsdp')
- grad_shared_in: float32 [768, 4096], P('fsdp', 'ctx')
- grad_shared_down: float32 [2048, 768], P('fsdp', 'ctx')
- grad_expert_in: float32 [16, 768, 4096], P('fsdp', 'ctx')
- grad_expert_down: float32 [16, 2048, 768], P('fsdp', 'ctx')
The draws below stay inside these ranges and needn't reach their ends.
Inputs may be any that keep to these rules, and one draw needn't show every extreme that they name: `lengths`: some sequence has exactly 2048 valid tokens. `routes`: each token names 2 different experts; in the rows of one device (aligned blocks of 256) no expert is named by more than 64 rows, a bound that some block reaches.
All inputs are finite; a program needn't handle non-finite values.
Results may differ from the reference program's by a relative error of at most 0.023.
Values may be sent and summed in bfloat16 or wider, within the bound.
No kernel may reach another device: no remote copies, remote signals or barrier semaphores. Data moves between devices by JAX's collectives and lax.ppermute only.
A program may use at most 256 MiB of HBM per device.

```python
import math
import jax
import jax.numpy as jnp
import numpy as np
from jax import lax

D = 768
HEADS = 12
HEAD_DIM = 64
FF = 2048
EXPERTS = 16
TOP = 2
SEQ_DEV = 256
BATCH = 4
SEQ = 2048
CAP = 64


def draw_lengths(key, part):
    first_key, second_key = jax.random.split(key)
    drawn = jax.random.randint(first_key, (BATCH,), SEQ // 4, SEQ + 1)
    longest = jax.random.randint(second_key, (), 0, BATCH)
    return jnp.where(jnp.arange(BATCH) == longest, SEQ, drawn).astype(jnp.int32)


def steps_of(rng, dims, shards, smallest, largest):
    gain = 1.0
    for axis_at, shards_of in shards:
        heights = jax.random.uniform(jax.random.fold_in(jax.random.fold_in(rng, 6), axis_at), (shards_of,), jnp.float32, smallest / len(shards), largest / len(shards))
        gain = gain * jnp.repeat(jnp.exp(heights), dims[axis_at] // shards_of).reshape((-1,) + (1,) * (len(dims) - 1 - axis_at))
    return gain


def deal_out(own_key, own, number, rows, number_of, top, limit, slope):
    order = jax.random.permutation(own_key, number_of)
    heavy_load, usual = portions_of(number_of, rows * top, limit, slope, True), portions_of(number_of, rows * top, limit, slope, False)
    places = jnp.arange(number_of)

    def named(sizes, turn):
        used = int((sizes > 0).sum())
        fixed = max(1, used // 4)
        moved = fixed + (places - fixed + turn * (used - fixed)) % max(1, number_of - fixed)
        return jnp.zeros((number_of,), jnp.int32).at[order[jnp.where(places < fixed, places, moved)]].set(jnp.asarray(sizes, jnp.int32))

    sizes = jnp.where(number % 4 == 0, named(heavy_load, number // 4), named(usual, number - number // 4 - 1))
    mixed = jax.random.permutation(jax.random.fold_in(own, 3), number_of)
    giver, sink = mixed[0:number_of // 2 * 2:2], mixed[1:number_of // 2 * 2:2]
    slack = jnp.minimum(sizes[giver] - 1, limit - sizes[sink]) // 2
    slack = jnp.where((giver == order[0]) | (sink == order[0]) | (sizes[sink] == 0), 0, jnp.maximum(slack, 0))
    moved = jax.random.randint(jax.random.fold_in(own, 4), (number_of // 2,), 0, 1 << 20) % (slack + 1)
    sizes = sizes.at[giver].add(-moved).at[sink].add(moved)
    labels = jnp.searchsorted(jnp.cumsum(sizes), jnp.arange(rows * top), side="right").astype(jnp.int32)
    grid = labels.reshape(top, rows).T
    grid = grid[jax.random.permutation(jax.random.fold_in(own, 1), rows)]
    turn = jax.random.randint(jax.random.fold_in(own, 2), (rows, 1), 0, top)
    return jnp.take_along_axis(grid, (jnp.arange(top)[None, :] + turn) % top, axis=1)


def portions_of(amount, total, limit, lean, full):
    loads = [(1 << 20) // math.isqrt(grade ** lean) + 1 for grade in range(1, amount + 1)]
    largest = limit if full else min(limit, max(-(-total // amount), total * loads[0] // sum(loads)))
    least = 1 if total - largest >= amount - 1 else 0
    counts, surplus = [largest] + [least] * (amount - 1), total - largest - least * (amount - 1)
    while surplus > 0:
        candidates = [i for i in range(1, amount) if counts[i] < largest] or [i for i in range(1, amount) if counts[i] < limit]
        pool, budget = sum([loads[i] for i in candidates]), surplus
        for i in candidates:
            addition = min(limit - counts[i], max(1, budget * loads[i] // pool), surplus)
            counts[i] = counts[i] + addition
            surplus = surplus - addition
    return np.array(counts)


def bell_draw(key, shape, scale, most, cuts=(), held_as=jnp.bfloat16):
    result = jax.random.normal(key, shape, jnp.float32) * scale
    if len(cuts) > 0:
        result = steps_of(key, shape, cuts, -0.22, 0.18) * result
    return jnp.clip(result, min=-most, max=most).astype(held_as)


def setup_inputs(seed: int = 0) -> dict:
    key_list = jax.random.split(jax.random.key(seed), 14)
    inputs = bell_draw(key_list[0], (BATCH, SEQ, D), 1.0, 6.0, ((0, 4), (1, 8)))
    gain_attn = jnp.clip(1.0 + 0.1 * jax.random.normal(key_list[1], (D,), jnp.float32), 0.5, 1.5).astype(jnp.bfloat16)
    w_qkv = bell_draw(key_list[2], (D, 3 * D), D ** -0.5, 0.21875, ((0, 4),))
    w_out = bell_draw(key_list[3], (D, D), (max(1, D * 32 // SEQ)) ** -0.5, 1.75, ((0, 4),))
    gain_ffn = jnp.clip(1.0 + 0.1 * jax.random.normal(key_list[4], (D,), jnp.float32), 0.5, 1.5).astype(jnp.bfloat16)
    w_shared_in = bell_draw(key_list[5], (D, 2 * FF), D ** -0.5, 0.21875, ((0, 4),))
    w_shared_down = bell_draw(key_list[6], (FF, D), FF ** -0.5, 0.125, ((0, 4),))
    w_expert_in = bell_draw(key_list[7], (EXPERTS, D, 2 * FF), D ** -0.5, 0.21875, ((0, 4),))
    w_expert_down = bell_draw(key_list[8], (EXPERTS, FF, D), FF ** -0.5, 0.125, ((0, 4),))
    lengths = draw_lengths(jax.random.fold_in(key_list[13], 71), 0)
    routes_keys = jax.random.split(jax.random.fold_in(key_list[10], 1), BATCH * SEQ // SEQ_DEV)
    routes_turns = jax.random.permutation(jax.random.fold_in(key_list[10], 3), BATCH * SEQ // SEQ_DEV)
    routes = jax.vmap(lambda own, number: deal_out(jax.random.fold_in(key_list[10], 2), own, number, SEQ_DEV, EXPERTS, TOP, CAP, 1))(routes_keys, routes_turns).reshape((BATCH, SEQ, TOP))
    gates = jnp.clip(0.2 + 0.8 * jax.random.uniform(key_list[11], (BATCH, SEQ, TOP), jnp.float32) ** steps_of(key_list[11], (BATCH, SEQ, TOP), ((0, 4), (1, 8)), -0.2, 0.2), 0.2, 1.0)
    cotangent = bell_draw(key_list[12], (BATCH, SEQ, D), 1.0, 6.0, ((0, 4), (1, 8)))
    return dict(inputs=inputs, gain_attn=gain_attn, w_qkv=w_qkv, w_out=w_out, gain_ffn=gain_ffn, w_shared_in=w_shared_in, w_shared_down=w_shared_down, w_expert_in=w_expert_in, w_expert_down=w_expert_down, lengths=lengths, routes=routes, gates=gates, cotangent=cotangent)


EPSILON = 1e-05
MASKED_SCORE = -1e+30
ROPE_BASE = 10000.0
HIGHEST = lax.Precision.HIGHEST

@jax.custom_vjp
def low(v):
    return lax.optimization_barrier(v.astype(jnp.bfloat16)).astype(jnp.float32)

@jax.custom_vjp
def low_back(v):
    return v

def low_keep(v):
    return (low(v), None)

def low_pass(kept, grad):
    return (grad,)

def back_keep(v):
    return (v, None)

def back_low(kept, grad):
    return (low(grad),)
low.defvjp(low_keep, low_pass)
low_back.defvjp(back_keep, back_low)

def rms_norm(values, gain_value):
    factor = lax.rsqrt(lax.optimization_barrier(jnp.mean(values * values, axis=-1, keepdims=True)) + EPSILON)
    return values * factor * gain_value

def rope_tables(positions, head_size):
    half_dim = head_size // 2
    frequency = jnp.power(jnp.float32(ROPE_BASE), -(2.0 * jnp.arange(half_dim, dtype=jnp.float32)) / head_size)
    angles = positions.astype(jnp.float32)[:, None] * frequency[None, :]
    return (jnp.cos(angles), jnp.sin(angles))

def rotate(values, cosine_table, sine_table):
    half_dim = values.shape[-1] // 2
    lower_half = values[..., :half_dim]
    upper_half = values[..., half_dim:]
    cos_wide = cosine_table[:, None, :]
    sin_wide = sine_table[:, None, :]
    return jnp.concatenate([lower_half * cos_wide - upper_half * sin_wide, upper_half * cos_wide + lower_half * sin_wide], axis=-1)

def swiglu(gate_up):
    half_ff = gate_up.shape[-1] // 2
    return jax.nn.silu(gate_up[..., :half_ff]) * gate_up[..., half_ff:]

def attend(query_seq, key_seq, value_seq, seq_length):
    seq_len = query_seq.shape[0]
    blk_rows = math.gcd(512, seq_len)
    key_pos = jnp.arange(seq_len, dtype=jnp.int32)

    def one_block(block_args):
        query_blk, first_row = block_args
        scores = jnp.einsum('qhd,khd->hqk', query_blk, key_seq, precision=HIGHEST) * HEAD_DIM ** (-0.5)
        scores = low_back(scores)
        query_pos = first_row + jnp.arange(blk_rows, dtype=jnp.int32)
        allowed = (key_pos[None, :] <= query_pos[:, None]) & (key_pos[None, :] < seq_length)
        scores = jnp.where(allowed[None], scores, MASKED_SCORE)
        probabilities = low(jax.nn.softmax(scores, axis=-1))
        mixed = jnp.einsum('hqk,khd->qhd', probabilities, value_seq, precision=HIGHEST)
        return mixed.reshape(blk_rows, -1)
    block_count = seq_len // blk_rows
    starts = jnp.arange(block_count, dtype=jnp.int32) * blk_rows
    blocks = query_seq.reshape(block_count, blk_rows, query_seq.shape[1], query_seq.shape[2])
    return lax.map(jax.checkpoint(one_block), (blocks, starts)).reshape(seq_len, -1)

def expert_apply(expert_args):
    rows_in, weight_in, weight_down = expert_args
    gate_up = low_back(jnp.dot(rows_in, weight_in, precision=HIGHEST, preferred_element_type=jnp.float32))
    hidden = low(swiglu(gate_up))
    return low_back(low(jnp.dot(hidden, weight_down, precision=HIGHEST, preferred_element_type=jnp.float32)))

def layer(residual_in, gain_one, weight_qkv, weight_out, gain_two, shared_in, shared_down, expert_in, expert_down, live_rows, lengths, targets, gates):
    batch_n, seq_len, model_width = residual_in.shape
    attn_in = low(rms_norm(residual_in, gain_one))
    qkv = low_back(jnp.einsum('bsd,df->bsf', attn_in, weight_qkv, precision=HIGHEST))
    cosine_table, sine_table = rope_tables(jnp.arange(seq_len, dtype=jnp.int32), HEAD_DIM)
    split_shape = (batch_n, seq_len, HEADS, HEAD_DIM)
    queries = low(rotate(qkv[..., :model_width].reshape(split_shape), cosine_table, sine_table))
    keys_rot = low(rotate(qkv[..., model_width:2 * model_width].reshape(split_shape), cosine_table, sine_table))
    values_b = low(qkv[..., 2 * model_width:].reshape(split_shape))
    attended = lax.map(lambda group: attend(group[0], group[1], group[2], group[3]), (queries, keys_rot, values_b, lengths))
    attended = low_back(low(attended))
    hidden_state = residual_in + low_back(jnp.einsum('bsd,de->bse', attended, weight_out, precision=HIGHEST))
    ffn_in = low(rms_norm(hidden_state, gain_two))
    shared_gu = low_back(jnp.einsum('bsd,df->bsf', ffn_in, shared_in, precision=HIGHEST))
    shared_out = low_back(jnp.einsum('bsf,fd->bsd', low(swiglu(shared_gu)), shared_down, precision=HIGHEST))
    flat_in = ffn_in.reshape(batch_n * seq_len, model_width)
    slot_total = EXPERTS * (batch_n * seq_len // SEQ_DEV) * CAP
    buffer_rows = jnp.zeros((slot_total, model_width), jnp.float32).at[targets.reshape(-1)].add(jnp.repeat(flat_in, TOP, axis=0))
    buffer_rows = low_back(buffer_rows).reshape(EXPERTS, -1, model_width)
    expert_out = lax.map(jax.checkpoint(expert_apply), (buffer_rows, expert_in, expert_down)).reshape(-1, model_width)
    picked = expert_out[targets]
    moe_out = lax.optimization_barrier(jnp.sum(gates.reshape(batch_n * seq_len, TOP, 1) * picked, axis=1)).reshape(batch_n, seq_len, model_width)
    return live_rows * (hidden_state + shared_out + moe_out)

def reference(inputs, gain_attn, w_qkv, w_out, gain_ffn, w_shared_in, w_shared_down, w_expert_in, w_expert_down, lengths, routes, gates, cotangent):
    batch_n, seq_len, model_width = inputs.shape
    block_count = batch_n * seq_len // SEQ_DEV
    live_rows = (jnp.arange(seq_len, dtype=jnp.int32)[None, :] < lengths[:, None]).astype(jnp.float32)[:, :, None]
    block_routes = routes.reshape(block_count, SEQ_DEV * TOP).astype(jnp.int32)
    one_hot = (block_routes[:, :, None] == jnp.arange(EXPERTS, dtype=jnp.int32)[None, None, :]).astype(jnp.int32)
    before = jnp.cumsum(one_hot, axis=1) - one_hot
    slot_number = lax.optimization_barrier(jnp.sum(before * one_hot, axis=2))
    block_ids = jnp.arange(block_count, dtype=jnp.int32)[:, None]
    targets = (block_routes * (block_count * CAP) + block_ids * CAP + slot_number).reshape(batch_n * seq_len, TOP).astype(jnp.int32)
    gate_values = gates.astype(jnp.float32)

    def forward_fn(residual_in, gain_one, weight_qkv, weight_out, gain_two, shared_in, shared_down, expert_in, expert_down):
        return layer(residual_in, gain_one, weight_qkv, weight_out, gain_two, shared_in, shared_down, expert_in, expert_down, live_rows, lengths, targets, gate_values)
    output, pull_back = jax.vjp(forward_fn, inputs.astype(jnp.float32), gain_attn.astype(jnp.float32), w_qkv.astype(jnp.float32), w_out.astype(jnp.float32), gain_ffn.astype(jnp.float32), w_shared_in.astype(jnp.float32), w_shared_down.astype(jnp.float32), w_expert_in.astype(jnp.float32), w_expert_down.astype(jnp.float32))
    grads = pull_back(cotangent.astype(jnp.float32))
    return (output.astype(jnp.bfloat16), grads[0], grads[1], grads[2], grads[3], grads[4], grads[5], grads[6], grads[7], grads[8])
```

```python
import functools

import jax
import jax.numpy as jnp
from jax import lax
from jax.experimental import pallas as pl
from jax.experimental.pallas import tpu as pltpu
from jax.sharding import PartitionSpec as P

HEADS = 12
HEAD_DIM = 64
EXPERTS = 16
TOP = 2
CAP = 64
HEAD_GROUPS = 4

EPSILON = 1e-05
MASKED_SCORE = -1e30
ROPE_BASE = 10000.0

BF = jnp.bfloat16
F32 = jnp.float32


def dot(lhs, rhs, lhs_dim=1, rhs_dim=0):
    return lax.dot_general(
        lhs, rhs, (((lhs_dim,), (rhs_dim,)), ((), ())), preferred_element_type=F32
    )


def shape_of(shape, dtype=BF):
    return jax.ShapeDtypeStruct(tuple(shape), dtype)


SMEM = pl.BlockSpec(memory_space=pltpu.SMEM)
VMEM = pl.BlockSpec(memory_space=pltpu.VMEM)


def swap(value, mask, axis="ctx"):
    if mask == 0:
        return value
    size = lax.axis_size(axis)
    return lax.ppermute(value, axis, [(i, i ^ mask) for i in range(size)])


def link_bits(flip):
    bits = []
    bit = 2
    while bit < lax.axis_size("ctx"):
        bits.append(bit)
        bit *= 2
    return bits[::-1] if flip else bits


def stack_masks(flip):
    masks = [0]
    for bit in link_bits(flip) + [1]:
        masks = masks + [mask | bit for mask in masks]
    return masks


def plane_gather(block, flip):
    pieces = {0: block}
    for bit in link_bits(flip) + [1]:
        for mask in list(pieces):
            pieces[mask | bit] = swap(pieces[mask], bit)
    return pieces


def plane_reduce(keep, send, flip):
    bits = [1] + link_bits(flip)[::-1]
    for at, bit in enumerate(bits):
        got = swap(send, bit)
        if at + 1 == len(bits):
            return keep[0], got[0]
        half = keep.shape[0] // 2
        send = (keep[half:].astype(F32) + got[half:].astype(F32)).astype(BF)
        keep = (keep[:half].astype(F32) + got[:half].astype(F32)).astype(BF)


def add(terms):
    return sum(term.astype(F32) for term in terms)


def axis_pieces(block, axis="fsdp"):
    return [swap(block, mask, axis) for mask in range(lax.axis_size(axis))]


def stack_rows(pieces, axis="fsdp"):
    size = len(pieces)
    index = lax.axis_index(axis)
    whole = jnp.zeros((size,) + pieces[0].shape, pieces[0].dtype)
    for mask in range(size):
        whole = lax.dynamic_update_slice_in_dim(whole, pieces[mask][None], index ^ mask, 0)
    return whole


def scatter_sum(parts, axis="fsdp"):
    size = lax.axis_size(axis)
    index = lax.axis_index(axis)
    total = lax.dynamic_index_in_dim(parts, index, 0, keepdims=False).astype(F32)
    for mask in range(1, size):
        part = lax.dynamic_index_in_dim(parts, index ^ mask, 0, keepdims=False)
        total = total + swap(part, mask, axis).astype(F32)
    return total


def sum_everywhere(value):
    for axis in ("fsdp", "ctx"):
        mask = 1
        while mask < lax.axis_size(axis):
            value = value + swap(value, mask, axis)
            mask *= 2
    return value


def live_of(tok, own, length):
    pos = own * tok + lax.broadcasted_iota(jnp.int32, (tok, 1), 0)
    return (pos < length).astype(F32)


def one_hot(target_ref, c, first, count):
    tok = target_ref.shape[0]
    slots = first + lax.broadcasted_iota(jnp.int32, (tok, count), 1)
    return (target_ref[:, c : c + 1] == slots).astype(BF)


def dispatch_kernel(local_experts, scal, routes_ref, gates_ref, cot_ref, target_ref, live_ref, *outs):
    own, plane, length = scal[0], scal[1], scal[2]
    tok = cot_ref.shape[0]
    experts = lax.broadcasted_iota(jnp.int32, (tok, EXPERTS), 1)
    hots = [(routes_ref[:, c : c + 1] == experts).astype(F32) for c in range(TOP)]
    row = lax.broadcasted_iota(jnp.int32, (tok, tok), 0)
    col = lax.broadcasted_iota(jnp.int32, (tok, tok), 1)
    earlier = dot((col < row).astype(BF), sum(hots).astype(BF))
    for c in range(TOP):
        slot = jnp.sum(earlier * hots[c], axis=1, keepdims=True).astype(jnp.int32)
        expert = routes_ref[:, c : c + 1]
        relative = ((expert // local_experts) ^ plane) * local_experts + expert % local_experts
        target_ref[:, c : c + 1] = relative * CAP + slot
    dsum = cot_ref[...].astype(F32) * live_of(tok, own, length)
    live_ref[...] = dsum.astype(BF)
    gated = [(gates_ref[:, c : c + 1] * dsum).astype(BF) for c in range(TOP)]
    rows = local_experts * CAP
    for at, out in enumerate(outs):
        out[...] = sum(
            dot(one_hot(target_ref, c, at * rows, rows), gated[c], 0, 0) for c in range(TOP)
        ).astype(BF)


def dispatch(scal, routes, gates, cotangent, owners, local_experts):
    tok, width = cotangent.shape
    return pl.pallas_call(
        functools.partial(dispatch_kernel, local_experts),
        in_specs=[SMEM, VMEM, VMEM, VMEM],
        out_specs=[VMEM] * (2 + owners),
        out_shape=[shape_of((tok, TOP), jnp.int32), shape_of((tok, width))]
        + [shape_of((local_experts * CAP, width))] * owners,
        name="dispatch",
    )(scal, routes, gates, cotangent)


def prep_kernel(groups, fsdp, scal, gain_ref, cos_ref, sin_ref, *refs):
    plane = scal[1]
    w_refs, rest = refs[:fsdp], refs[fsdp:]
    count = (len(rest) - 10) // 1
    x_refs = rest[:count]
    q_ref, k_ref, v_ref, a_ref, f_ref, wq_ref, wk_ref, wv_ref, rq_ref, rk_ref = rest[count:]
    heads = q_ref.shape[0]
    shard = w_refs[0].shape[0]
    tok = x_refs[0].shape[0]
    cols = heads * HEAD_DIM
    for mask in range(fsdp):
        rows = pl.ds(pl.multiple_of((plane ^ mask) * shard, shard), shard)
        for at, ref in enumerate((wq_ref, wk_ref, wv_ref)):
            ref[rows, :] = w_refs[mask][:, at * cols : (at + 1) * cols]
    row = lax.broadcasted_iota(jnp.int32, (cols, cols), 0)
    col = lax.broadcasted_iota(jnp.int32, (cols, cols), 1)
    half = HEAD_DIM // 2
    low = (col % HEAD_DIM) < half
    turn = jnp.where(low & (row == col + half), -1.0, 0.0) + jnp.where(
        jnp.logical_not(low) & (row == col - half), 1.0, 0.0
    )
    turn = turn.astype(BF)
    rq_ref[...] = dot(wq_ref[...], turn).astype(BF)
    rk_ref[...] = dot(wk_ref[...], turn).astype(BF)
    scale = BF(HEAD_DIM ** (-0.5))
    for at in range(count):
        rows = slice(at * tok, (at + 1) * tok)
        x = x_refs[at][...].astype(F32)
        factor = lax.rsqrt(jnp.mean(x * x, axis=-1, keepdims=True) + EPSILON)
        a = (x * factor * gain_ref[...]).astype(BF)
        cosine, sine = cos_ref[rows, :], sin_ref[rows, :]
        k = (dot(a, wk_ref[...]) * cosine + dot(a, rk_ref[...]) * sine).astype(BF)
        v = dot(a, wv_ref[...]).astype(BF)
        if at < groups:
            a_ref[rows, :] = a
            f_ref[rows, :] = factor
            q = (dot(a, wq_ref[...]) * cosine + dot(a, rq_ref[...]) * sine).astype(BF) * scale
        for h in range(heads):
            lanes = slice(h * HEAD_DIM, (h + 1) * HEAD_DIM)
            k_ref[h, rows, :] = k[:, lanes]
            v_ref[h, rows, :] = v[:, lanes]
            if at < groups:
                q_ref[h, rows, :] = q[:, lanes]


def prep(scal, gain, cosine, sine, weights, pieces, groups, heads):
    tok, width = pieces[0].shape
    count = len(pieces)
    cols = heads * HEAD_DIM
    mine, keys = groups * tok, count * tok
    outs = [
        shape_of((heads, mine, HEAD_DIM)),
        shape_of((heads, keys, HEAD_DIM)),
        shape_of((heads, keys, HEAD_DIM)),
        shape_of((mine, width)),
        shape_of((mine, 1), F32),
        shape_of((width, cols)),
        shape_of((width, cols)),
        shape_of((width, cols)),
    ]
    return pl.pallas_call(
        functools.partial(prep_kernel, groups, len(weights)),
        in_specs=[SMEM] + [VMEM] * (3 + len(weights) + count),
        out_specs=[VMEM] * len(outs),
        out_shape=outs,
        scratch_shapes=[pltpu.VMEM((width, cols), BF)] * 2,
        name="prep",
    )(scal, gain, cosine, sine, *weights, *pieces)


def attend_kernel(share, tok, scal, q_ref, k_ref, v_ref, *outs):
    groups = pl.num_programs(0)
    own, length = scal[0], scal[2]
    o_ref, ot_ref, lse_ref = outs
    q_blk = own ^ (pl.program_id(0) * share)
    full_end = jnp.minimum(q_blk, length // tok)
    end = jnp.minimum(q_blk, (length - 1) // tok) + 1
    heads = q_ref.shape[0]
    size = q_ref.shape[2]

    def tile(key_blk, state, masked):
        mask = key_blk ^ own
        base = pl.multiple_of(((mask % share) * groups + mask // share) * tok, tok)
        if masked:
            key_pos = key_blk * tok + lax.broadcasted_iota(jnp.int32, (tok, tok), 0)
            query_pos = q_blk * tok + lax.broadcasted_iota(jnp.int32, (tok, tok), 1)
            allowed = (key_pos <= query_pos) & (key_pos < length)
        after = []
        for h in range(heads):
            top, total, acc = state[h]
            keys = k_ref[h, pl.ds(base, tok), :]
            values = v_ref[h, pl.ds(base, tok), :]
            scores = dot(keys, q_ref[h], 1, 1)
            if masked:
                scores = jnp.where(allowed, scores, MASKED_SCORE)
            new_top = jnp.maximum(top, jnp.max(scores, axis=0, keepdims=True))
            grown = jnp.exp(scores - new_top)
            factor = jnp.exp(top - new_top)
            total = total * factor + jnp.sum(grown, axis=0, keepdims=True)
            acc = acc * factor + dot(values, grown.astype(BF), 0, 0)
            after.append((new_top, total, acc))
        return tuple(after)

    state = tuple(
        (
            jnp.full((1, tok), MASKED_SCORE, F32),
            jnp.zeros((1, tok), F32),
            jnp.zeros((size, tok), F32),
        )
        for _ in range(heads)
    )
    state = lax.fori_loop(0, full_end, lambda i, s: tile(i, s, False), state)
    state = lax.fori_loop(full_end, end, lambda i, s: tile(i, s, True), state)
    for h in range(heads):
        top, total, acc = state[h]
        out = acc / total
        ot_ref[h] = out
        lse_ref[h] = top + jnp.log(total)
        o_ref[:, h * size : (h + 1) * size] = out.T.astype(BF)


def attend(scal, q, k, v, share, groups, tok):
    heads, _, size = q.shape
    keys = k.shape[1]
    whole = pl.BlockSpec((heads, keys, size), lambda i, s: (0, 0, 0))
    return pl.pallas_call(
        functools.partial(attend_kernel, share, tok),
        grid_spec=pltpu.PrefetchScalarGridSpec(
            num_scalar_prefetch=1,
            grid=(groups,),
            in_specs=[
                pl.BlockSpec((heads, tok, size), lambda i, s: (0, i, 0)),
                whole,
                whole,
            ],
            out_specs=[
                pl.BlockSpec((tok, heads * size), lambda i, s: (i, 0)),
                pl.BlockSpec((heads, size, tok), lambda i, s: (0, 0, i)),
                pl.BlockSpec((heads, 1, tok), lambda i, s: (0, 0, i)),
            ],
        ),
        out_shape=[
            shape_of((groups * tok, heads * size)),
            shape_of((heads, size, groups * tok), F32),
            shape_of((heads, 1, groups * tok), F32),
        ],
        name="attend",
    )(scal, q, k, v)


def attend_back_kernel(share, tok, scal, q_ref, do_ref, k_ref, v_ref, ot_ref, lse_ref, *outs):
    dq_ref, own_ref = outs[:2]
    send_refs, (dk_ref, dv_ref) = outs[2:-2], outs[-2:]
    groups = pl.num_programs(0)
    own, length = scal[0], scal[2]
    q_blk = own ^ (pl.program_id(0) * share)
    full_end = jnp.minimum(q_blk, length // tok)
    end = jnp.minimum(q_blk, (length - 1) // tok) + 1
    heads = q_ref.shape[0]
    size = q_ref.shape[2]

    @pl.when(pl.program_id(0) == 0)
    def _():
        dk_ref[...] = jnp.zeros_like(dk_ref)
        dv_ref[...] = jnp.zeros_like(dv_ref)

    grads, dots = [], []
    for h in range(heads):
        grad = do_ref[:, h * size : (h + 1) * size]
        grads.append(grad)
        dots.append(jnp.sum(grad.astype(F32).T * ot_ref[h], axis=0, keepdims=True))

    def tile(key_blk, state, masked):
        mask = key_blk ^ own
        base = pl.multiple_of(((mask % share) * groups + mask // share) * tok, tok)
        if masked:
            key_pos = key_blk * tok + lax.broadcasted_iota(jnp.int32, (tok, tok), 0)
            query_pos = q_blk * tok + lax.broadcasted_iota(jnp.int32, (tok, tok), 1)
            allowed = (key_pos <= query_pos) & (key_pos < length)
        after = []
        for h in range(heads):
            keys = k_ref[h, pl.ds(base, tok), :]
            values = v_ref[h, pl.ds(base, tok), :]
            prob = jnp.exp(dot(keys, q_ref[h], 1, 1) - lse_ref[h])
            if masked:
                prob = jnp.where(allowed, prob, 0.0)
            grad_prob = dot(values, grads[h], 1, 1)
            grad_score = (prob * (grad_prob - dots[h])).astype(BF)
            dv_ref[h, pl.ds(base, tok), :] += dot(prob.astype(BF), grads[h])
            dk_ref[h, pl.ds(base, tok), :] += dot(grad_score, q_ref[h])
            after.append(state[h] + dot(keys, grad_score, 0, 0))
        return tuple(after)

    state = tuple(jnp.zeros((size, tok), F32) for _ in range(heads))
    state = lax.fori_loop(0, full_end, lambda i, s: tile(i, s, False), state)
    state = lax.fori_loop(full_end, end, lambda i, s: tile(i, s, True), state)
    for h in range(heads):
        dq_ref[:, h * size : (h + 1) * size] = state[h].T

    @pl.when(pl.program_id(0) == groups - 1)
    def _():
        mine = own_ref.shape[0]
        for at, ref in enumerate((dk_ref, dv_ref)):
            for h in range(heads):
                lanes = slice((at * heads + h) * size, (at * heads + h + 1) * size)
                own_ref[:, lanes] = ref[h, :mine, :]
                for rest, send in enumerate(send_refs):
                    first = (rest + 1) * mine
                    send[:, lanes] = ref[h, first : first + mine, :].astype(BF)


def attend_back(scal, q, do, k, v, ot, lse, share, groups, tok):
    heads, _, size = q.shape
    keys = k.shape[1]
    cols = heads * size
    mine = groups * tok
    whole = pl.BlockSpec((heads, keys, size), lambda i, s: (0, 0, 0))
    flat = pl.BlockSpec((mine, 2 * cols), lambda i, s: (0, 0))
    return pl.pallas_call(
        functools.partial(attend_back_kernel, share, tok),
        grid_spec=pltpu.PrefetchScalarGridSpec(
            num_scalar_prefetch=1,
            grid=(groups,),
            in_specs=[
                pl.BlockSpec((heads, tok, size), lambda i, s: (0, i, 0)),
                pl.BlockSpec((tok, cols), lambda i, s: (i, 0)),
                whole,
                whole,
                pl.BlockSpec((heads, size, tok), lambda i, s: (0, 0, i)),
                pl.BlockSpec((heads, 1, tok), lambda i, s: (0, 0, i)),
            ],
            out_specs=[pl.BlockSpec((tok, cols), lambda i, s: (i, 0))] + [flat] * share,
            scratch_shapes=[pltpu.VMEM((heads, keys, size), F32)] * 2,
        ),
        out_shape=[shape_of((mine, cols), F32), shape_of((mine, 2 * cols), F32)]
        + [shape_of((mine, 2 * cols))] * (share - 1),
        name="attend_back",
    )(scal, q, do, k, v, ot, lse)


def out_kernel(groups, fsdp, rows_each, scal, x_ref, gain_ref, target_ref, *refs):
    plane, group = scal[1], scal[3]
    o_refs = refs[:groups]
    w_refs = refs[groups : groups + fsdp]
    h_ref, f_ref, in_ref, w_ref = refs[groups + fsdp : groups + fsdp + 4]
    outs = refs[groups + fsdp + 4 :]
    shard = w_refs[0].shape[0]
    cols = o_refs[0].shape[1]
    for mask in range(fsdp):
        w_ref[pl.ds(pl.multiple_of((plane ^ mask) * shard, shard), shard), :] = w_refs[mask][...]
    h = x_ref[...].astype(F32)
    for at in range(groups):
        first = pl.multiple_of((group ^ at) * cols, cols)
        h = h + dot(o_refs[at][...], w_ref[pl.ds(first, cols), :])
    h_ref[...] = h
    factor = lax.rsqrt(jnp.mean(h * h, axis=-1, keepdims=True) + EPSILON)
    f_ref[...] = factor
    ffn_in = (h * factor * gain_ref[...]).astype(BF)
    in_ref[...] = ffn_in
    for at, out in enumerate(outs):
        place = sum(one_hot(target_ref, c, at * rows_each, rows_each) for c in range(TOP))
        out[...] = dot(place, ffn_in, 0, 0).astype(BF)


def out_project(scal, x, gain, target, o_pieces, weights, owners, rows_each):
    tok, width = x.shape
    groups, fsdp = len(o_pieces), len(weights)
    return pl.pallas_call(
        functools.partial(out_kernel, groups, fsdp, rows_each),
        in_specs=[SMEM] + [VMEM] * (3 + groups + fsdp),
        out_specs=[VMEM] * (4 + owners),
        out_shape=[
            shape_of((tok, width), F32),
            shape_of((tok, 1), F32),
            shape_of((tok, width)),
            shape_of((width, width)),
        ]
        + [shape_of((rows_each, width))] * owners,
        name="out_project",
    )(scal, x, gain, target, *o_pieces, *weights)


def mid_kernel(groups, owners, scal, cot_ref, gain_ref, target_ref, h_ref, f_ref, w_ref, *refs):
    own, length, group = scal[0], scal[2], scal[3]
    keep_ref, got_ref = refs[:2]
    row_refs = refs[2 : 2 + owners]
    dh_ref, dao_ref, gain_out = refs[2 + owners : 5 + owners]
    do_refs = refs[5 + owners :]
    tok, width = h_ref.shape
    rows = row_refs[0].shape[0]
    db = keep_ref[...].astype(F32) + got_ref[...].astype(F32)
    for at in range(owners):
        place = sum(one_hot(target_ref, c, at * rows, rows) for c in range(TOP))
        db = db + dot(place, row_refs[at][...])
    h, factor = h_ref[...], f_ref[...]
    gain_out[...] = jnp.sum(db * (h * factor), axis=0, keepdims=True)
    scaled = gain_ref[...] * db
    inner = jnp.mean(scaled * h, axis=-1, keepdims=True)
    dsum = cot_ref[...].astype(F32) * live_of(tok, own, length)
    dh = dsum + factor * scaled - h * (factor * factor * factor * inner)
    dh_ref[...] = dh
    dao = dh.astype(BF)
    dao_ref[...] = dao
    cols = do_refs[0].shape[1]
    for at, ref in enumerate(do_refs):
        first = pl.multiple_of((group ^ at) * cols, cols)
        ref[...] = dot(dao, w_ref[pl.ds(first, cols), :], 1, 1).astype(BF)


def mid_back(scal, cot, gain, target, h, factor, w, db_terms, rows, groups, cols):
    tok, width = h.shape
    owners = len(rows)
    return pl.pallas_call(
        functools.partial(mid_kernel, groups, owners),
        in_specs=[SMEM] + [VMEM] * (8 + owners),
        out_specs=[VMEM] * (3 + groups),
        out_shape=[
            shape_of((tok, width), F32),
            shape_of((tok, width)),
            shape_of((1, width), F32),
        ]
        + [shape_of((tok, cols))] * groups,
        name="mid_back",
    )(scal, cot, gain, target, h, factor, w, *db_terms, *rows)


def out_grad_kernel(groups, masks, scal, dao_ref, *refs):
    own, group = scal[0], scal[3]
    o_refs = refs[:groups]
    keep_ref, send_ref, part_ref = refs[groups:]
    half, _, size, _ = keep_ref.shape
    for at in range(groups):
        part_ref[...] = dot(dao_ref[...], o_refs[at][...], 0, 0).astype(BF)
        for k, mask in enumerate(masks):
            first = pl.multiple_of((own ^ mask) * size, size)
            out = keep_ref if k < half else send_ref
            out[k % half, group ^ at] = part_ref[pl.ds(first, size), :]


def out_grad(scal, dao, o_pieces, masks):
    tok, width = dao.shape
    groups = len(o_pieces)
    count = len(masks)
    cols = o_pieces[0].shape[1]
    half = shape_of((count // 2, groups, width // count, cols))
    return pl.pallas_call(
        functools.partial(out_grad_kernel, groups, masks),
        in_specs=[SMEM] + [VMEM] * (1 + groups),
        out_specs=[VMEM] * 2,
        out_shape=[half, half],
        scratch_shapes=[pltpu.VMEM((width, cols), BF)],
        name="out_grad",
    )(scal, dao, *o_pieces)


def turn_back(values):
    half = HEAD_DIM // 2
    parts = []
    for first in range(0, values.shape[1], HEAD_DIM):
        parts.append(values[:, first + half : first + HEAD_DIM])
        parts.append(-values[:, first : first + half])
    return jnp.concatenate(parts, axis=1)


def qkv_back_kernel(groups, share, dq_ref, own_ref, *refs):
    got_refs, refs = refs[: share - 1], refs[share - 1 :]
    cos_ref, sin_ref, a_ref, f_ref, wq_ref, wk_ref, wv_ref = refs[:7]
    x_refs, refs = refs[7 : 7 + groups], refs[7 + groups :]
    din_ref, sends, grad_ref, gain_ref = refs[0], refs[1:groups], refs[groups], refs[groups + 1]
    dall_ref = refs[groups + 2]
    tok, width = din_ref.shape
    cols = dq_ref.shape[1]
    unit = cols // share
    scale = HEAD_DIM ** (-0.5)
    gain_sum = jnp.zeros((1, width), F32)
    for at in range(groups):
        rows = slice(at * tok, (at + 1) * tok)
        cosine, sine = cos_ref[rows, :], sin_ref[rows, :]
        dkv = own_ref[rows, :]
        for got in got_refs:
            dkv = dkv + got[rows, :].astype(F32)
        dq = dq_ref[rows, :] * scale
        dk, dv = dkv[:, :cols], dkv[:, cols:]
        dq = (dq * cosine + turn_back(dq * sine)).astype(BF)
        dk = (dk * cosine + turn_back(dk * sine)).astype(BF)
        dv = dv.astype(BF)
        for k, part in enumerate((dq, dk, dv)):
            dall_ref[k, rows, :] = part
        din = dot(dq, wq_ref[...], 1, 1) + dot(dk, wk_ref[...], 1, 1) + dot(dv, wv_ref[...], 1, 1)
        x = x_refs[at][...].astype(F32)
        gain_sum = gain_sum + jnp.sum(din * (x * f_ref[rows, :]), axis=0, keepdims=True)
        if at == 0:
            din_ref[...] = din
        else:
            sends[at - 1][...] = din.astype(BF)
    gain_ref[...] = gain_sum
    for k in range(3):
        grad = dot(a_ref[...], dall_ref[k], 0, 0).astype(BF)
        for r in range(share):
            grad_ref[r, k] = grad[:, r * unit : (r + 1) * unit]


def qkv_back(dq, dkv, got, cosine, sine, a, factor, weights, x_pieces, share):
    groups = len(x_pieces)
    tok, width = x_pieces[0].shape
    mine, cols = dq.shape
    return pl.pallas_call(
        functools.partial(qkv_back_kernel, groups, share),
        in_specs=[VMEM] * (2 + len(got) + 7 + groups),
        out_specs=[VMEM] * (groups + 2),
        out_shape=[shape_of((tok, width), F32)]
        + [shape_of((tok, width))] * (groups - 1)
        + [shape_of((share, 3, width, cols // share)), shape_of((1, width), F32)],
        scratch_shapes=[pltpu.VMEM((3, mine, cols), BF)],
        name="qkv_back",
    )(dq, dkv, *got, cosine, sine, a, factor, *weights, *x_pieces)


ROWS = 64


def ffn_kernel(count, carried, turn, scal, *refs):
    row_refs, dy_refs = refs[:count], refs[count : 2 * count]
    wg_ref, wu_ref, wd_ref = refs[2 * count : 2 * count + 3]
    keep_ref, send_ref, he_ref, dgu_ref, rows_ref, dys_ref = refs[2 * count + 3 + carried :]
    width = rows_ref.shape[-1]
    hidden = wd_ref.shape[1]

    def put(ref, value):
        ref[:, 0, 0] = value.reshape(count, ROWS, value.shape[-1])

    rows = jnp.concatenate([ref[0] for ref in row_refs], axis=0)
    dy = jnp.concatenate([ref[0] for ref in dy_refs], axis=0)
    put(rows_ref, rows)
    put(dys_ref, dy)
    gate = dot(rows, wg_ref[0])
    up = dot(rows, wu_ref[0])
    dhe = dot(dy, wd_ref[0], 1, 1)
    sigma = jax.nn.sigmoid(gate)
    silu = gate * sigma
    put(he_ref, (silu * up).astype(BF))
    dg = (dhe * up * (sigma * (1.0 + gate * (1.0 - sigma)))).astype(BF)
    du = (dhe * silu).astype(BF)
    dgu_ref[:, 0, 0, :, :hidden] = dg.reshape(count, ROWS, hidden)
    dgu_ref[:, 0, 0, :, hidden:] = du.reshape(count, ROWS, hidden)
    drow = (dot(dg, wg_ref[0], 1, 1) + dot(du, wu_ref[0], 1, 1)).astype(BF)
    drow = drow.reshape(count, ROWS, width)
    half = count // 2
    for at, k in enumerate(turn):
        (keep_ref if at < half else send_ref)[at % half, 0, 0] = drow[k]


def ffn(scal, pieces, dys, dy_first, w_in, w_down, hidden, first, total, carry, turn):
    count = len(pieces)
    blocks, _, width = pieces[0].shape
    experts = w_in.shape[0]
    steps = blocks // experts

    def stacked(depth, last, base):
        return pl.BlockSpec(
            (depth, 1, 1, ROWS, last), lambda e, i, s: (0, base + i, e, 0, 0)
        )

    def shape(depth, many, last):
        return shape_of((depth, many, experts, ROWS, last))

    half = count // 2
    carried = len(carry)
    base_in = 1 + 2 * count + 3
    return pl.pallas_call(
        functools.partial(ffn_kernel, count, carried, turn),
        grid_spec=pltpu.PrefetchScalarGridSpec(
            num_scalar_prefetch=1,
            grid=(experts, steps),
            in_specs=[
                pl.BlockSpec((1, ROWS, width), lambda e, i, s: (i * experts + e, 0, 0))
            ]
            * count
            + [
                pl.BlockSpec((1, ROWS, width), lambda e, i, s: (dy_first + i * experts + e, 0, 0))
            ]
            * count
            + [
                pl.BlockSpec((1, width, hidden), lambda e, i, s: (e, 0, s[0])),
                pl.BlockSpec((1, width, hidden), lambda e, i, s: (e, 0, s[1])),
                pl.BlockSpec((1, hidden, width), lambda e, i, s: (e, s[0], 0)),
            ]
            + [pl.BlockSpec(memory_space=pl.ANY)] * carried,
            out_specs=[
                stacked(half, width, 0),
                stacked(half, width, 0),
                stacked(count, hidden, first),
                stacked(count, 2 * hidden, first),
                stacked(count, width, first),
                stacked(count, width, first),
            ],
        ),
        out_shape=[
            shape(half, steps, width),
            shape(half, steps, width),
            shape(count, total, hidden),
            shape(count, total, 2 * hidden),
            shape(count, total, width),
            shape(count, total, width),
        ],
        input_output_aliases={base_in + at: 2 + at for at in range(carried)},
        name="ffn",
    )(scal, *pieces, *dys, w_in, w_in, w_down, *carry)


def ffn_grads_kernel(
    scal, wd_ref, he_ref, dgu_ref, rows_ref, dys_ref, keep_ref, send_ref, gd_ref, gi_ref, acc_ref
):
    count, many, _, rows_n, width = rows_ref.shape
    total = count * many * rows_n
    hidden = wd_ref.shape[1]
    step = pl.program_id(1)
    he = he_ref[...].reshape(total, hidden)
    ye = dot(he, wd_ref[0]).astype(BF).reshape(count, many, 1, rows_n, width)
    keep_ref[...] = ye[: count // 2]
    send_ref[...] = ye[count // 2 :]
    gd = dot(he, dys_ref[...].reshape(total, width), 0, 0)
    gi = dot(rows_ref[...].reshape(total, width), dgu_ref[...].reshape(total, 2 * hidden), 0, 0)

    @pl.when(step == 0)
    def _():
        gd_ref[0] = gd
        acc_ref[...] = gi

    @pl.when(step > 0)
    def _():
        gd_ref[0] += gd
        acc_ref[...] += gi

    @pl.when(step == pl.num_programs(1) - 1)
    def _():
        gi_ref[:, 0] = acc_ref[...].astype(BF).reshape(count, width // count, 2 * hidden)


def ffn_grads(scal, w_down, carry, hidden):
    he, dgu, rows, dys = carry
    count, total, experts, _, width = rows.shape
    many = max(1, min(total, 2048 // (count * ROWS)))

    def stacked(depth, last):
        return pl.BlockSpec((depth, many, 1, ROWS, last), lambda e, i, s: (0, i, e, 0, 0))

    half = shape_of((count // 2, total, experts, ROWS, width))
    return pl.pallas_call(
        ffn_grads_kernel,
        grid_spec=pltpu.PrefetchScalarGridSpec(
            num_scalar_prefetch=1,
            grid=(experts, total // many),
            in_specs=[
                pl.BlockSpec((1, hidden, width), lambda e, i, s: (e, s[0], 0)),
                stacked(count, hidden),
                stacked(count, 2 * hidden),
                stacked(count, width),
                stacked(count, width),
            ],
            out_specs=[
                stacked(count // 2, width),
                stacked(count // 2, width),
                pl.BlockSpec((1, hidden, width), lambda e, i, s: (e, 0, 0)),
                pl.BlockSpec((count, 1, width // count, 2 * hidden), lambda e, i, s: (0, e, 0, 0)),
            ],
            scratch_shapes=[pltpu.VMEM((width, 2 * hidden), F32)],
        ),
        out_shape=[
            half,
            half,
            shape_of((experts, hidden, width), F32),
            shape_of((count, experts, width // count, 2 * hidden)),
        ],
        name="ffn_grads",
    )(scal, w_down, he, dgu, rows, dys)


def place_kernel(in_ref, out_ref):
    count, _, _, both = in_ref.shape
    hidden = both // 2
    for at in range(count):
        out_ref[0, :, at * hidden : (at + 1) * hidden] = in_ref[at, 0, :, :hidden].astype(F32)
        first = (count + at) * hidden
        out_ref[0, :, first : first + hidden] = in_ref[at, 0, :, hidden:].astype(F32)


def place_experts(got):
    count, experts, rows, both = got.shape
    return pl.pallas_call(
        place_kernel,
        grid=(experts,),
        in_specs=[pl.BlockSpec((count, 1, rows, both), lambda e: (0, e, 0, 0))],
        out_specs=pl.BlockSpec((1, rows, count * both), lambda e: (e, 0, 0)),
        out_shape=shape_of((experts, rows, count * both), F32),
        name="place_experts",
    )(got)


def combine_kernel(owners, scal, h_ref, target_ref, gates_ref, keep_ref, got_ref, *refs):
    own, length = scal[0], scal[2]
    row_refs, out_ref = refs[:owners], refs[owners]
    tok = h_ref.shape[0]
    rows = row_refs[0].shape[0]
    total = h_ref[...] + keep_ref[...].astype(F32) + got_ref[...].astype(F32)
    for at in range(owners):
        for c in range(TOP):
            picked = dot(one_hot(target_ref, c, at * rows, rows), row_refs[at][...])
            total = total + gates_ref[:, c : c + 1] * picked
    out_ref[...] = (live_of(tok, own, length) * total).astype(BF)


def combine(scal, h, target, gates, terms, rows):
    return pl.pallas_call(
        functools.partial(combine_kernel, len(rows)),
        in_specs=[SMEM] + [VMEM] * (5 + len(rows)),
        out_specs=VMEM,
        out_shape=shape_of(h.shape),
        name="combine",
    )(scal, h, target, gates, *terms, *rows)


def per_device(
    inputs,
    gain_attn,
    w_qkv,
    w_out,
    gain_ffn,
    w_shared_in,
    w_shared_down,
    w_expert_in,
    w_expert_down,
    lengths,
    routes,
    gates,
    cotangent,
):
    tok, width = inputs.shape[1], inputs.shape[2]
    ctx, fsdp = lax.axis_size("ctx"), lax.axis_size("fsdp")
    own, plane = lax.axis_index("ctx"), lax.axis_index("fsdp")
    groups = HEAD_GROUPS
    share = ctx // groups
    head_group = own // share
    heads = HEADS // groups
    cols = heads * HEAD_DIM
    local_experts = EXPERTS // fsdp
    d_shard = width // fsdp
    x = inputs[0]
    scal = jnp.stack([own, plane, lengths[0], head_group]).astype(jnp.int32)

    order = [group * share + rest for rest in range(share) for group in range(groups)]
    x_pieces = [swap(x, mask) for mask in order[:groups]]
    for rest in range(1, share):
        x_pieces += [swap(piece, rest) for piece in x_pieces[:groups]]
    qkv_cols = lax.dynamic_slice_in_dim(
        w_qkv.reshape(d_shard, 3, width), head_group * cols, cols, 2
    ).reshape(d_shard, 3 * cols)
    qkv_pieces = axis_pieces(qkv_cols)
    gains = stack_rows(axis_pieces(jnp.stack([gain_attn, gain_ffn]))).astype(F32)
    gain_one = gains[:, 0].reshape(1, width)
    gain_two = gains[:, 1].reshape(1, width)
    out_pieces = axis_pieces(w_out)

    rows_each = local_experts * CAP
    cot, gate_values = cotangent[0], gates[0]
    target, d_shared, *dy_blocks = dispatch(
        scal, routes[0], gate_values, cot, fsdp, local_experts
    )
    dy_blocks = [swap(dy_blocks[at], at, "fsdp") for at in range(fsdp)]

    ff_shard = w_shared_down.shape[0]
    ff_part = ff_shard // ctx
    hidden = w_expert_down.shape[1] // ctx
    shared_cols = lax.dynamic_index_in_dim(
        w_shared_in.reshape(d_shard, 2, fsdp, ctx, ff_part), own, 3, keepdims=False
    ).reshape(d_shard, 2 * hidden)
    shared_in = stack_rows(axis_pieces(shared_cols)).reshape(1, width, 2 * hidden)
    shared_down = stack_rows(
        axis_pieces(lax.dynamic_slice_in_dim(w_shared_down, own * ff_part, ff_part, 0))
    ).reshape(1, hidden, width)

    blocks = own ^ jnp.array(order, jnp.int32)
    positions = (blocks[:, None] * tok + jnp.arange(tok, dtype=jnp.int32)[None, :]).reshape(-1)
    frequency = jnp.power(
        F32(ROPE_BASE), -(2.0 * jnp.arange(HEAD_DIM // 2, dtype=F32)) / HEAD_DIM
    )
    angles = positions.astype(F32)[:, None] * frequency[None, :]
    cosine = jnp.tile(jnp.cos(angles), (1, 2 * heads))
    sine = jnp.tile(jnp.sin(angles), (1, 2 * heads))
    q_h, k_h, v_h, attn_in, x_factor, *w_qkv_own = prep(
        scal, gain_one, cosine, sine, qkv_pieces, x_pieces, groups, heads
    )
    o_group, o_t, lse = attend(scal, q_h, k_h, v_h, share, groups, tok)
    o_pieces = [swap(o_group[at * tok : (at + 1) * tok], at * share) for at in range(groups)]
    h, factor, ffn_in, w_out_full, *row_blocks = out_project(
        scal, x, gain_two, target, o_pieces, out_pieces, fsdp, rows_each
    )

    def as_blocks(array):
        return array.reshape(-1, ROWS, width)

    shared_blocks = tok // ROWS
    first_dy = jnp.concatenate([as_blocks(d_shared), as_blocks(dy_blocks[0])], axis=0)
    later_dy = jnp.concatenate([as_blocks(block) for block in dy_blocks[1:]], axis=0)
    first_dy, later_dy, k_h = lax.optimization_barrier((first_dy, later_dy, k_h))
    first_dy = plane_gather(first_dy, True)
    later_dy = plane_gather(later_dy, False)

    many = 1 if fsdp <= 4 else 4
    sets = [[0]] + [list(range(at, min(at + many, fsdp))) for at in range(1, fsdp, many)]
    flips = [bool(at % 2) for at in range(len(sets))]
    shared_scal = jnp.array([0, 1], jnp.int32)
    expert_scal = jnp.stack([own, own + ctx]).astype(jnp.int32)

    shared_rows = plane_gather(as_blocks(ffn_in), True)
    expert_rows = []
    for at, members in enumerate(sets):
        got = [as_blocks(swap(row_blocks[mask], mask, "fsdp")) for mask in members]
        block = got[0] if len(got) == 1 else jnp.concatenate(got, axis=0)
        expert_rows.append(plane_gather(block, flips[at]))

    masks = stack_masks(False)

    def turn(flip):
        return tuple(masks.index(mask) for mask in stack_masks(flip))

    keep, send, *shared_carry = ffn(
        shared_scal,
        [shared_rows[mask] for mask in masks],
        [first_dy[mask] for mask in masks],
        0,
        shared_in,
        shared_down,
        hidden,
        0,
        shared_blocks,
        [],
        turn(True),
    )
    db_terms = plane_reduce(keep, send, True)
    d_rows = [None] * fsdp
    carry = []
    for at, members in enumerate(sets):
        dys, first = (first_dy, shared_blocks) if at == 0 else (
            later_dy,
            (members[0] - 1) * local_experts,
        )
        keep, send, *carry = ffn(
            expert_scal,
            [expert_rows[at][mask] for mask in masks],
            [dys[mask] for mask in masks],
            first,
            w_expert_in,
            w_expert_down,
            hidden,
            members[0],
            fsdp,
            carry,
            turn(flips[at]),
        )
        block = add(plane_reduce(keep, send, flips[at])).astype(BF)
        for k, mask in enumerate(members):
            d_rows[mask] = swap(block[k].reshape(rows_each, width), mask, "fsdp")

    d_hidden, d_attn_out, gain_two_part, *do_pieces = mid_back(
        scal, cot, gain_two, target, h, factor, w_out_full, [
            term.reshape(tok, width) for term in db_terms
        ], d_rows, groups, cols
    )
    do_group = jnp.concatenate(
        [swap(do_pieces[at], at * share) for at in range(groups)], axis=0
    )

    s_keep, s_send, grad_sd, grad_si = ffn_grads(shared_scal, shared_down, shared_carry, hidden)
    keep, send, grad_ed, grad_ei = ffn_grads(expert_scal, w_expert_down, carry, hidden)
    shared_terms = plane_reduce(s_keep, s_send, False)
    block = add(plane_reduce(keep, send, False)).astype(BF)
    out_rows = [
        swap(block[mask].reshape(rows_each, width), mask, "fsdp") for mask in range(fsdp)
    ]
    output = combine(
        scal, h, target, gate_values, [t.reshape(tok, width) for t in shared_terms], out_rows
    )[None]
    out_masks = stack_masks(False)
    grad_out = add(plane_reduce(*out_grad(scal, d_attn_out, o_pieces, out_masks), False))
    grad_out = jnp.swapaxes(grad_out.astype(BF), 1, 2).reshape(fsdp, d_shard, width // ctx)
    grad_out = scatter_sum(grad_out)

    dq, dkv, *sends = attend_back(scal, q_h, do_group, k_h, v_h, o_t, lse, share, groups, tok)
    got = [swap(part, rest + 1) for rest, part in enumerate(sends)]
    mine = groups * tok
    *d_in_parts, grad_qkv, gain_one_part = qkv_back(
        dq,
        dkv,
        got,
        cosine[:mine],
        sine[:mine],
        attn_in,
        x_factor,
        w_qkv_own,
        x_pieces[:groups],
        share,
    )
    d_in = add(
        [d_in_parts[0]] + [swap(d_in_parts[at], at * share) for at in range(1, groups)]
    )
    gains_sum = sum_everywhere(jnp.concatenate([gain_one_part, gain_two_part], axis=0))
    residual = x.astype(F32)
    scaled = gain_one * d_in
    x_own = x_factor[:tok]
    inner = jnp.mean(scaled * residual, axis=-1, keepdims=True)
    grad_inputs = (d_hidden + x_own * scaled - residual * (x_own * x_own * x_own * inner))[None]

    def to_ctx(parts_of):
        return lax.all_to_all(parts_of, "ctx", split_axis=0, concat_axis=0, tiled=True)

    final_ei = place_experts(to_ctx(grad_ei))
    si = scatter_sum(grad_si.reshape(fsdp, d_shard, 2 * hidden)).astype(BF)
    final_si = place_columns(si.reshape(d_shard, 2 * fsdp, ff_part), w_shared_in.shape[1])
    sd = scatter_sum(grad_sd[0].astype(BF).reshape(fsdp, ff_part, width)).astype(BF)
    sd = to_ctx(jnp.swapaxes(sd.reshape(ff_part, ctx, width // ctx), 0, 1))
    final_sd = sd.reshape(ff_shard, width // ctx).astype(F32)

    bit = share // 2
    index = own % share
    while bit >= 1:
        upper = (index // bit) % 2
        kept = lax.dynamic_slice_in_dim(grad_qkv, upper * bit, bit, 0)
        sent = lax.dynamic_slice_in_dim(grad_qkv, (1 - upper) * bit, bit, 0)
        grad_qkv = (kept.astype(F32) + swap(sent, bit).astype(F32)).astype(BF)
        bit //= 2
    grad_qkv = grad_qkv[0].reshape(3, fsdp, d_shard, cols // share)
    grad_qkv = scatter_sum(jnp.swapaxes(grad_qkv, 0, 1)).astype(BF)
    final_qkv = place_units(grad_qkv)

    def own_rows(total):
        return lax.dynamic_slice_in_dim(total, plane * d_shard, d_shard, 0)

    return (
        output,
        grad_inputs,
        own_rows(gains_sum[0]),
        final_qkv,
        grad_out,
        own_rows(gains_sum[1]),
        final_si,
        final_sd,
        final_ei,
        grad_ed,
    )


def place_units(units):
    ctx = lax.axis_size("ctx")
    own = lax.axis_index("ctx")
    got = []
    for m in range(3):
        inverse = pow(ctx % 3, -1, 3)
        k = ((m - own) * inverse) % 3
        unit = lax.dynamic_index_in_dim(units, k, 0, keepdims=False)
        got.append(lax.ppermute(unit, "ctx", [((3 * i + m) % ctx, i) for i in range(ctx)]))
    return jnp.concatenate(got, axis=1).astype(F32)


def place_columns(si, columns):
    ctx = lax.axis_size("ctx")
    rows, many, part = si.shape
    if many >= ctx:
        each = many // ctx
        si = jnp.transpose(si.reshape(rows, ctx, each, part), (1, 2, 0, 3))
        got = lax.all_to_all(si, "ctx", split_axis=0, concat_axis=0, tiled=True)
        return jnp.transpose(got, (2, 1, 0, 3)).reshape(rows, -1).astype(F32)
    whole = lax.all_gather(si, "ctx", axis=2).reshape(rows, columns)
    size = columns // ctx
    return lax.dynamic_slice_in_dim(whole, lax.axis_index("ctx") * size, size, 1).astype(F32)


def solution(mesh):
    row, col = P("fsdp", "ctx", None), P("fsdp", "ctx")
    in_specs = (
        row,
        P("fsdp"),
        P("fsdp", None),
        P("fsdp", None),
        P("fsdp"),
        P("fsdp", None),
        P("fsdp", None),
        P("fsdp", None, None),
        P("fsdp", None, None),
        P("fsdp"),
        row,
        row,
        row,
    )
    out_specs = (row, row, P("fsdp"), col, col, P("fsdp"), col, col, row, row)
    return jax.shard_map(
        per_device, mesh=mesh, in_specs=in_specs, out_specs=out_specs, check_vma=False
    )
```
